32 devices in a mesh: fact: 4 (over z), dim: 8 (over y, x, core).
Axes of the slice: x: 2, y: 2, z: 4, core: 2. Of those that a mesh axis runs over, the one named last changes fastest.
Arguments:
- facts: bfloat16 [4096, 512], P(('fact', 'dim')), may hold values from -6 to 6
- dims: bfloat16 [4096, 512], P(('fact', 'dim')), may hold values from -6 to 6
- tiles: bfloat16 [1024, 128, 128], P(('fact', 'dim')), may hold values from -0.125 to 0.125
- links: int32 [1024, 2], P(('fact', 'dim')), may hold values from 0 to 31, as said below
- link_count: int32 [32], P(('fact', 'dim')), may hold values from 8 to 32, as said below
- block_table: int32 [32], replicated, may hold values from 0 to 2
- w_self: bfloat16 [512, 512], replicated, may hold values from -0.25 to 0.25
- w_tables: bfloat16 [3, 512, 512], replicated, may hold values from -0.25 to 0.25
- cot: bfloat16 [4096, 512], P(('fact', 'dim')), may hold values from -6 to 6
Outputs:
- fact_out: bfloat16 [4096, 512], P(('fact', 'dim'))
- grad_dims: float32 [4096, 512], P(('fact', 'dim'))
- grad_w_self: float32 [512, 512], replicated
- grad_w_tables: float32 [3, 512, 512], replicated
The draws below stay inside these ranges and needn't reach their ends.
Inputs may be any that keep to these rules, and one draw needn't show every extreme that they name: On device k = f * 8 + d (f, d its fact and dim indices), links[l,0] is a fact block among those of rows f * 128 * 8 to (f + 1) * 128 * 8 - 1, and links[l,1] is a dimension block held by a device with dim index d, i.e. links[l,1] % 8 == d. Slots beyond the device's count hold such indices too and are padding. `link_count`: some device has all 32 slots live and some device exactly 8.
All inputs are finite; a program needn't handle non-finite values.
Results may differ from the reference program's by a relative error of at most 0.017.
Values may be sent and summed in bfloat16 or wider, within the bound.
A program may use at most 64 MiB of HBM per device.

```python
import jax
import jax.numpy as jnp
from jax import lax

D = 512
TABLES = 3
BLOCK = 128
FACT_DEV = 128
DIM_DEV = 128
LINKS_DEV = 32
NF = 4096
ND = 4096
LINKS = 1024
DBLOCKS = 32
N_FACT = 4
N_DIM = 8


def draw_links(key, part):
    devices = N_FACT * N_DIM
    first, second, third = jax.random.split(key, 3)
    device = jnp.arange(devices, dtype=jnp.int32)
    fact_index = device // N_DIM
    dim_index = device % N_DIM
    fact_blocks = FACT_DEV * N_DIM // BLOCK
    per_owner = DIM_DEV // BLOCK
    fact_off = jax.random.randint(first, (devices, LINKS_DEV), 0, fact_blocks)
    holder = jax.random.randint(second, (devices, LINKS_DEV), 0, N_FACT)
    within = jax.random.randint(third, (devices, LINKS_DEV), 0, per_owner)
    slot = jnp.arange(LINKS_DEV, dtype=jnp.int32)
    first_dev = (device[:, None] == 0) & (slot[None, :] == 0)
    last_dev = (device[:, None] == devices - 1) & (slot[None, :] == 0)
    fact_off = jnp.where(first_dev, 0, jnp.where(last_dev, fact_blocks - 1, fact_off))
    holder = jnp.where(first_dev, 0, jnp.where(last_dev, N_FACT - 1, holder))
    within = jnp.where(first_dev, 0, jnp.where(last_dev, per_owner - 1, within))
    fact_blk = fact_index[:, None] * fact_blocks + fact_off
    dim_blk = (holder * N_DIM + dim_index[:, None]) * per_owner + within
    return jnp.stack([fact_blk, dim_blk], axis=-1).reshape(devices * LINKS_DEV, 2).astype(jnp.int32)


def draw_link_count(key, part):
    devices = N_FACT * N_DIM
    first, second, third = jax.random.split(key, 3)
    lowest = LINKS_DEV // 4
    counts = jax.random.randint(first, (devices,), lowest, LINKS_DEV + 1)
    busiest = jax.random.randint(second, (), 0, devices)
    lightest = (busiest + 1 + jax.random.randint(third, (), 0, devices - 1)) % devices
    device = jnp.arange(devices, dtype=jnp.int32)
    counts = jnp.where(device == busiest, LINKS_DEV, counts)
    counts = jnp.where(device == lightest, lowest, counts)
    return counts.astype(jnp.int32)


def place_ends(values, key, least, largest):
    shape = values.shape
    index_at = [jax.random.randint(jax.random.fold_in(key, axis), (), 0, shape[axis]) for axis in range(len(shape))]
    values = values.at[tuple(index_at)].set(least)
    longest = shape.index(max(shape))
    index_at[longest] = (index_at[longest] + 1) % shape[longest]
    return values.at[tuple(index_at)].set(largest)


def level_of(rng, shape, cuts, low, top_value):
    loudness, own = 1.0, jax.random.fold_in(rng, 6)
    for position, blocks in cuts:
        heights = jnp.exp(jax.random.uniform(jax.random.fold_in(own, position), (blocks,), jnp.float32, low / len(cuts), top_value / len(cuts)))
        loudness = loudness * jnp.repeat(heights, shape[position] // blocks).reshape([-1 if axis == position else 1 for axis in range(len(shape))])
    return loudness


def centred(rng, shape, spread, most, cuts=(), held_as=jnp.bfloat16):
    loudness = level_of(rng, shape, cuts, -0.22, 0.18) if cuts else 1.0
    entries = jax.random.normal(rng, shape, jnp.float32) * spread * loudness
    return jnp.minimum(jnp.maximum(entries, -most), most).astype(held_as)


def setup_inputs(seed: int = 0) -> dict:
    streams_of = jax.random.split(jax.random.key(seed), 10)
    facts = centred(streams_of[0], (NF, D), 1.0, 6.0, ((0, 32),))
    dims = centred(streams_of[1], (ND, D), 1.0, 6.0, ((0, 32),))
    tiles = centred(streams_of[2], (LINKS, BLOCK, BLOCK), (5 * LINKS_DEV * BLOCK * BLOCK // (8 * FACT_DEV)) ** -0.5, 0.125, ((0, 32),))
    links = draw_links(jax.random.fold_in(streams_of[9], 71), 0)
    link_count = draw_link_count(jax.random.fold_in(streams_of[9], 71), 0)
    block_table = place_ends(jax.random.randint(streams_of[5], (DBLOCKS,), 0, TABLES), jax.random.fold_in(streams_of[5], 1), 0, TABLES - 1).astype(jnp.int32)
    w_self = centred(streams_of[6], (D, D), D ** -0.5, 0.25)
    w_tables = centred(streams_of[7], (TABLES, D, D), D ** -0.5, 0.25)
    cot = centred(streams_of[8], (NF, D), 1.0, 6.0, ((0, 32),))
    return dict(facts=facts, dims=dims, tiles=tiles, links=links, link_count=link_count, block_table=block_table, w_self=w_self, w_tables=w_tables, cot=cot)


def project_rows(rows, row_table, w_tables):
    acc = jnp.zeros((rows.shape[0], w_tables.shape[2]), jnp.float32)
    for table in range(TABLES):
        term = jnp.dot(rows, w_tables[table], preferred_element_type=jnp.float32)
        acc = acc + jnp.where(row_table[:, None] == table, term, jnp.float32(0.0))
    return acc


def reference(facts, dims, tiles, links, link_count, block_table, w_self, w_tables, cot):
    devices = N_FACT * N_DIM
    row_table = jnp.repeat(block_table, BLOCK)
    projected = project_rows(dims, row_table, w_tables).astype(jnp.bfloat16)
    slot = jnp.arange(LINKS, dtype=jnp.int32) % LINKS_DEV
    owner = jnp.arange(LINKS, dtype=jnp.int32) // LINKS_DEV
    live = (slot < link_count[owner]).astype(jnp.float32).reshape(devices, LINKS_DEV)
    tile_dev = tiles.reshape(devices, LINKS_DEV, BLOCK, BLOCK)
    link_dev = links.reshape(devices, LINKS_DEV, 2)
    proj_blocks = projected.reshape(ND // BLOCK, BLOCK, D)

    def forward_step(acc, xs):
        tile, link, alive = xs
        blocks = proj_blocks[link[:, 1]].astype(jnp.float32)
        contrib = jnp.einsum('lij,ljd->lid', tile.astype(jnp.float32), blocks) * alive[:, None, None]
        return acc.at[link[:, 0]].add(contrib), None

    agg, _ = lax.scan(forward_step, jnp.zeros((NF // BLOCK, BLOCK, D), jnp.float32), (tile_dev, link_dev, live))
    pre = jnp.dot(facts, w_self, preferred_element_type=jnp.float32) + agg.reshape(NF, D)
    fact_out = jax.nn.silu(pre).astype(jnp.bfloat16)
    sig = jax.nn.sigmoid(pre)
    grad_pre = (cot.astype(jnp.float32) * sig * (1.0 + pre * (1.0 - sig))).astype(jnp.bfloat16)
    grad_w_self = lax.dot_general(facts, grad_pre, (((0,), (0,)), ((), ())), preferred_element_type=jnp.float32) * (NF ** -0.5)
    grad_blocks = grad_pre.reshape(NF // BLOCK, BLOCK, D)

    def backward_step(acc, xs):
        tile, link, alive = xs
        blocks = grad_blocks[link[:, 0]].astype(jnp.float32)
        contrib = jnp.einsum('lji,ljd->lid', tile.astype(jnp.float32), blocks) * alive[:, None, None]
        return acc.at[link[:, 1]].add(contrib), None

    gsum, _ = lax.scan(backward_step, jnp.zeros((ND // BLOCK, BLOCK, D), jnp.float32), (tile_dev, link_dev, live))
    gsum_b = gsum.reshape(ND, D).astype(jnp.bfloat16)
    grad_dims = jnp.zeros((ND, D), jnp.float32)
    grads = []
    for table in range(TABLES):
        term = lax.dot_general(gsum_b, w_tables[table], (((1,), (1,)), ((), ())), preferred_element_type=jnp.float32)
        grad_dims = grad_dims + jnp.where(row_table[:, None] == table, term, jnp.float32(0.0))
        masked = jnp.where(row_table[:, None] == table, dims, jnp.zeros_like(dims))
        grads.append(lax.dot_general(masked, gsum_b, (((0,), (0,)), ((), ())), preferred_element_type=jnp.float32) * (ND ** -0.5))
    grad_w_tables = jnp.stack(grads)
    return (fact_out, grad_dims, grad_w_self, grad_w_tables)
```

```python
import functools

import jax
import jax.numpy as jnp
from jax import lax
from jax.experimental import pallas as pl
from jax.experimental.pallas import tpu as pltpu
from jax.sharding import PartitionSpec as P

MESH = pl.DeviceIdType.MESH
BF = jnp.bfloat16
F32 = jnp.float32
CORES = 2
STAGES = 4


def dot(a, b):
    return jnp.dot(a, b, preferred_element_type=F32)


def flip(x):
    return x.astype(F32).T.astype(BF)


def prep_kernel(dims_n, links_h, count_h, table_h, tiles_h, w_tables_h, adj, w_one, links, count, table, tiles, acc, sems):
    n_fact, n_dim = dims_n
    chips = n_dim // CORES
    block = tiles.shape[1]
    f = lax.axis_index("fact")
    d = lax.axis_index("dim")
    small = [
        pltpu.make_async_copy(table_h, table, sems.at[0]),
        pltpu.make_async_copy(links_h, links, sems.at[1]),
        pltpu.make_async_copy(count_h, count, sems.at[2]),
    ]
    load = pltpu.make_async_copy(tiles_h, tiles, sems.at[3])
    for copy in small:
        copy.start()
    load.start()
    acc[...] = jnp.zeros_like(acc)
    small[0].wait()
    own = table[f * n_dim + d]
    weight = pltpu.make_async_copy(w_tables_h.at[own], w_one, sems.at[4])
    weight.start()
    small[1].wait()
    small[2].wait()
    load.wait()

    def add(l, _):
        i = links[0, l] - f * n_dim
        row = lax.rem(i, CORES) * chips + lax.div(i, CORES)
        col = lax.div(links[1, l], n_dim)
        acc[row, col] += tiles[l].astype(F32)
        return 0

    lax.fori_loop(0, count[0], add, 0)
    for i in range(n_dim):
        for j in range(n_fact):
            adj[i * block : (i + 1) * block, j * block : (j + 1) * block] = acc[i, j].astype(BF)
    weight.wait()


def main_kernel(
    dims_n, table, adj, w_one, facts, dims, cot, w_self,
    fact_out, grad_dims, weights,
    proj, chunks, panel, adj_t, chunk_all, masked, pre, send1, recv1, mine, send2, recv2, gp, grad,
    send3, recv3, gs, gs_all, w_own, w_send, w_recv,
    a_s, a_r, f_s, f_r, b1_s, b1_r, b2_s, b2_r, c_s, c_r, m_s, m_r,
    d_s, d_r, e_s, e_r, w_s, w_r, z_s, z_r, p_s, p_r, q_s, q_r,
):
    n_fact, n_dim = dims_n
    chips = n_dim // CORES
    rows, width = facts.shape
    cut = width // STAGES
    tables = weights.shape[1] - 1
    depth = chunks.shape[1] // 2
    per = n_fact // (tables + 1)
    part = depth // per
    f = lax.axis_index("fact")
    d = lax.axis_index("dim")
    c = lax.div(d, CORES)
    k = lax.rem(d, CORES)
    o = 1 - k
    mate = c * CORES + o
    scale_f = float(rows * n_fact * n_dim) ** -0.5
    to_f = [lax.rem(f + j, n_fact) for j in range(n_fact)]
    from_f = [lax.rem(f + n_fact - j, n_fact) for j in range(n_fact)]
    to_c = [lax.rem(c + j, chips) for j in range(chips)]
    from_c = [lax.rem(c + chips - j, chips) for j in range(chips)]
    every = range(STAGES)
    far = sorted(range(1, n_fact), key=lambda j: abs(2 * j - n_fact))
    near = sorted(range(1, n_fact), key=lambda j: min(j, n_fact - j))
    order = list(range(1, chips)) + [0]
    rb = k * chips + c
    group = chips * rows

    def remote(src, dst, ss, rs, df, dd):
        return pltpu.make_async_remote_copy(
            src_ref=src, dst_ref=dst, send_sem=ss, recv_sem=rs,
            device_id=(df, dd), device_id_type=MESH,
        )

    def blk(i):
        return pl.ds(pl.multiple_of(i * rows, rows), rows)

    def grp(i):
        return pl.ds(pl.multiple_of(i * group, group), group)

    def unit(i):
        return pl.ds(pl.multiple_of(i * part, part), part)

    def cols(h):
        return slice(h * cut, (h + 1) * cut)

    def holder(h):
        return h % CORES

    def place(h, ff, cc):
        start = pl.multiple_of(cc * depth + lax.rem(ff, per) * part, part)
        return (h, lax.div(ff, per), pl.ds(start, part))

    def region(h, ff, cc):
        return weights.at[place(h, ff, cc)]

    def copy_a(h, j):
        return remote(proj.at[h], panel.at[h, blk(f)], a_s.at[h, j], a_r.at[h, j], to_f[j], d)

    def copy_f(j):
        to = lax.rem(d + j, n_dim)
        return remote(
            chunks.at[lax.div(to, CORES)], chunk_all.at[:, blk(rb)], f_s.at[j], f_r.at[j], f, to
        )

    def copy_1(h, j):
        at = blk(to_c[j])
        return remote(send1.at[h, at], recv1.at[h, at], b1_s.at[h, j], b1_r.at[h, j], f, mate)

    def copy_2(h, j):
        return remote(
            send2.at[h, j], recv2.at[h, j], b2_s.at[h, j], b2_r.at[h, j], f, to_c[j] * CORES + k
        )

    def copy_c(h, j):
        src = gp.at[h, blk(rb)]
        return remote(src, src, c_s.at[h, j], c_r.at[h, j], f, to_c[j] * CORES + k)

    def copy_m(h, j):
        src = gp.at[h, blk(k * chips + from_c[j])]
        return remote(src, src, m_s.at[h, j], m_r.at[h, j], f, mate)

    def copy_d(h, j):
        return remote(
            send3.at[h, j], recv3.at[h, j], d_s.at[h, j], d_r.at[h, j], to_f[j], d
        )

    def copy_e(h, j, source):
        return remote(
            gs.at[h], gs_all.at[h // CORES, blk(rb)], e_s.at[h, j], e_r.at[h, j, source],
            f, to_c[j] * CORES + holder(h),
        )

    def copy_w(h, j):
        return remote(
            w_send.at[h // CORES, j], w_recv.at[h // CORES, j], w_s.at[h, j], w_r.at[h, j],
            to_f[j], d,
        )

    def copy_z(h, j):
        src = region(h, f, c)
        return remote(src, src, z_s.at[h, j], z_r.at[h, j], to_f[j], d)

    def copy_p(h, i, j):
        src = region(h, from_f[i], c)
        return remote(src, src, p_s.at[h, i, j], p_r.at[h, i, j], f, to_c[j] * CORES + k)

    def copy_q(h, i, j):
        src = region(h, from_f[i], from_c[j])
        return remote(src, src, q_s.at[h, i, j], q_r.at[h, i, j], f, mate)

    barrier = pltpu.get_barrier_semaphore()
    for j in range(1, n_fact):
        pl.semaphore_signal(barrier, inc=1, device_id=(to_f[j], d), device_id_type=MESH)
    for j in range(1, n_dim):
        pl.semaphore_signal(
            barrier, inc=1, device_id=(f, lax.rem(d + j, n_dim)), device_id_type=MESH
        )
    both = dot(dims[...], w_one[...]).astype(BF)
    for h in every:
        proj[h] = both[:, cols(h)]
    pl.semaphore_wait(barrier, n_dim + n_fact - 2)

    for h in every:
        for j in far:
            copy_a(h, j).start()
    facts_t = flip(facts[...])
    dims_t = flip(dims[...])
    for i in range(chips):
        chunks[i, :depth] = facts_t[i * depth : (i + 1) * depth]
        chunks[i, depth:] = dims_t[i * depth : (i + 1) * depth]
    for j in range(1, n_dim):
        copy_f(j).start()
    for h in every:
        panel[h, blk(f), :] = proj[h]
        pre[h] = dot(facts[...], w_self[:, cols(h)])
    chunk_all[:, blk(rb)] = chunks[c]
    for i in range(n_dim):
        adj_t[:, i * rows : (i + 1) * rows] = flip(adj[i * rows : (i + 1) * rows, :])

    def forward(h):
        for j in far:
            copy_a(h, j).wait_recv()
        send1[h] = dot(adj[grp(o), :], panel[h]).astype(BF)
        for j in order:
            copy_1(h, j).start()
        mine[h] = dot(adj[grp(k), :], panel[h])

    def pair(h):
        for j in order:
            copy_1(h, j).wait_recv()
            at = blk(to_c[j])
            total = mine[h, at, :] + recv1[h, at, :].astype(F32)
            if j:
                send2[h, j] = total.astype(BF)
                copy_2(h, j).start()
            else:
                pre[h] += total

    def activate(h):
        total = pre[h]
        for j in range(1, chips):
            copy_2(h, j).wait_recv()
            total = total + recv2[h, j].astype(F32)
        sig = 1.0 / (1.0 + jnp.exp(-total))
        gp[h, blk(rb), :] = (
            cot[:, cols(h)].astype(F32) * sig * (1.0 + total * (1.0 - sig))
        ).astype(BF)
        for j in range(1, chips):
            copy_c(h, j).start()
        copy_m(h, 0).start()
        fact_out[:, cols(h)] = (total * sig).astype(BF)

    def share(h):
        for j in range(1, chips):
            copy_c(h, j).wait_recv()
            copy_m(h, j).start()
        grad[h] = dot(adj_t[:, grp(k)], gp[h, grp(k), :])

    def mask():
        for j in range(1, n_dim):
            copy_f(j).wait_recv()
        for i in range(n_dim):
            source = (i % chips) * CORES + i // chips
            name = table[f * n_dim + source]
            lanes = slice(i * rows, (i + 1) * rows)
            values = chunk_all[depth:, lanes].astype(F32)
            for t in range(tables):
                masked[t * depth : (t + 1) * depth, lanes] = (
                    values * (name == t).astype(F32)
                ).astype(BF)

    def backward(h):
        for j in range(chips):
            copy_m(h, j).wait_recv()
        grad[h] += dot(adj_t[:, grp(o)], gp[h, grp(o), :])
        for j in far:
            send3[h, j] = grad[h, blk(to_f[j]), :].astype(BF)
            copy_d(h, j).start()

        @pl.when(k == holder(h))
        def _():
            w_own[h // CORES, :depth, :] = dot(chunk_all[:depth, :], gp[h]) * scale_f

    def collect(h):
        total = grad[h, blk(f), :]
        for j in near:
            copy_d(h, j).wait_recv()
            total = total + recv3[h, j].astype(F32)
        rounded = total.astype(BF)
        gs[h] = rounded
        for j in range(1, chips):
            copy_e(h, j, k).start()

        @pl.when(k != holder(h))
        def _():
            copy_e(h, 0, 1 - holder(h)).start()

        @pl.when(k == holder(h))
        def _():
            gs_all[h // CORES, blk(rb), :] = gs[h]

        term = lax.dot_general(
            rounded, w_one[:, cols(h)], (((1,), (1,)), ((), ())), preferred_element_type=F32
        )
        if h:
            grad_dims[...] += term
        else:
            grad_dims[...] = term

    def table_weight(h):
        @pl.when(k == holder(h))
        def _():
            for j in range(1, chips):
                for source in range(CORES):
                    copy_e(h, j, source).wait_recv()
            copy_e(h, 0, 1 - holder(h)).wait_recv()
            own = h // CORES
            w_own[own, depth:, :] = dot(masked[...], gs_all[own]) * scale_f
            for j in far:
                w_send[own, j] = w_own[own, unit(to_f[j]), :].astype(BF)
                copy_w(h, j).start()

    def finish(h):
        @pl.when(k == holder(h))
        def _():
            own = h // CORES
            total = w_own[own, unit(f), :]
            for j in near:
                copy_w(h, j).wait_recv()
                total = total + w_recv[own, j].astype(F32)
            weights[place(h, f, c)] = total.astype(BF)
            for j in far:
                copy_z(h, j).start()
            for j in range(1, chips):
                copy_p(h, 0, j).start()
            copy_q(h, 0, 0).start()

    def relay(h):
        @pl.when(k == holder(h))
        def _():
            for i in near:
                copy_z(h, i).wait_recv()
                for j in range(1, chips):
                    copy_p(h, i, j).start()
                copy_q(h, i, 0).start()

    def hand(h):
        @pl.when(k == holder(h))
        def _():
            for i in [0] + near:
                for j in range(1, chips):
                    copy_p(h, i, j).wait_recv()
                    copy_q(h, i, j).start()

    tasks = [
        (0.0, forward), (1.5, pair), (5.2, activate), (8.8, share), (9.9, backward),
        (15.4, collect), (19.1, table_weight), (23.4, finish), (27.4, relay), (32.0, hand),
    ]
    step = 2.5
    plan = [(at + step * h, h, task) for at, task in tasks for h in every]
    plan.append((6.0, 0, lambda h: mask()))
    for _, h, task in sorted(plan, key=lambda item: item[:2]):
        task(h)

    for h in every:
        @pl.when(k != holder(h))
        def _():
            for i in range(n_fact):
                for j in range(chips):
                    copy_q(h, i, j).wait_recv()
            copy_e(h, 0, 1 - holder(h)).wait_send()

        @pl.when(k == holder(h))
        def _():
            for j in far:
                copy_w(h, j).wait_send()
                copy_z(h, j).wait_send()
            for i in range(n_fact):
                for j in range(chips):
                    if j:
                        copy_p(h, i, j).wait_send()
                    copy_q(h, i, j).wait_send()

        for j in far:
            copy_a(h, j).wait_send()
            copy_d(h, j).wait_send()
        for j in range(chips):
            copy_1(h, j).wait_send()
            copy_m(h, j).wait_send()
            if j:
                copy_2(h, j).wait_send()
                copy_c(h, j).wait_send()
                copy_e(h, j, k).wait_send()
    for j in range(1, n_dim):
        copy_f(j).wait_send()


def post_kernel(out_in, dims_in, weights, fact_out, grad_dims, w_self, w_tables, wide, sems):
    stages, tables, _, cut = weights.shape
    started = [
        pltpu.make_async_copy(out_in, fact_out, sems.at[tables]),
        pltpu.make_async_copy(dims_in, grad_dims, sems.at[tables + 1]),
    ]
    for copy in started:
        copy.start()
    for t in range(tables):
        for h in range(stages):
            wide[t, :, h * cut : (h + 1) * cut] = weights[h, t].astype(F32)
        copy = pltpu.make_async_copy(
            wide.at[t], w_tables.at[t - 1] if t else w_self, sems.at[t]
        )
        copy.start()
        started.append(copy)
    for copy in started:
        copy.wait()


def body(facts, dims, tiles, links, link_count, block_table, w_self, w_tables, cot):
    n_fact = lax.axis_size("fact")
    n_dim = lax.axis_size("dim")
    chips = n_dim // CORES
    rows, width = facts.shape
    block = tiles.shape[1]
    tables = w_tables.shape[0]
    depth = width // chips
    cut = width // STAGES
    part = depth * (tables + 1) // n_fact
    dims_n = (n_fact, n_dim)
    cells = n_fact * n_dim * rows * rows
    panes = (n_fact + n_dim) * rows * width
    grant = min(62 << 20, 4 * cells + 16 * panes + 8 * tables * width * width + (6 << 20))
    small = min(62 << 20, 8 * cells + 4 * width * width + 2 * tiles.size + (4 << 20))
    vmem = pl.BlockSpec(memory_space=pltpu.VMEM)
    smem = pl.BlockSpec(memory_space=pltpu.SMEM)
    anywhere = pl.BlockSpec(memory_space=pl.ANY)
    adj, w_one = pl.pallas_call(
        functools.partial(prep_kernel, dims_n),
        out_shape=(
            jax.ShapeDtypeStruct((n_dim * rows, n_fact * rows), BF),
            jax.ShapeDtypeStruct((width, width), BF),
        ),
        in_specs=[anywhere] * 5,
        out_specs=(vmem, vmem),
        scratch_shapes=[
            pltpu.SMEM(links.shape[::-1], jnp.int32),
            pltpu.SMEM(link_count.shape, jnp.int32),
            pltpu.SMEM(block_table.shape, jnp.int32),
            pltpu.VMEM(tiles.shape, BF),
            pltpu.VMEM((n_dim, n_fact, block, block), F32),
            pltpu.SemaphoreType.DMA((5,)),
        ],
        compiler_params=pltpu.CompilerParams(vmem_limit_bytes=small),
        name="prep",
    )(links.T, link_count, block_table, tiles, w_tables)

    def sems(*shape):
        return [pltpu.SemaphoreType.DMA((STAGES, *shape))] * 2

    held = STAGES // CORES
    fact_out, grad_dims, weights = pl.pallas_call(
        functools.partial(main_kernel, dims_n),
        out_shape=(
            jax.ShapeDtypeStruct((rows, width), BF),
            jax.ShapeDtypeStruct((rows, width), F32),
            jax.ShapeDtypeStruct((STAGES, tables + 1, width, cut), BF),
        ),
        in_specs=[smem] + [vmem] * 6,
        out_specs=(vmem, vmem, vmem),
        scratch_shapes=[
            pltpu.VMEM((STAGES, rows, cut), BF),
            pltpu.VMEM((chips, 2 * depth, rows), BF),
            pltpu.VMEM((STAGES, n_fact * rows, cut), BF),
            pltpu.VMEM((n_fact * rows, n_dim * rows), BF),
            pltpu.VMEM((2 * depth, n_dim * rows), BF),
            pltpu.VMEM((tables * depth, n_dim * rows), BF),
            pltpu.VMEM((STAGES, rows, cut), F32),
            pltpu.VMEM((STAGES, chips * rows, cut), BF),
            pltpu.VMEM((STAGES, chips * rows, cut), BF),
            pltpu.VMEM((STAGES, chips * rows, cut), F32),
            pltpu.VMEM((STAGES, chips, rows, cut), BF),
            pltpu.VMEM((STAGES, chips, rows, cut), BF),
            pltpu.VMEM((STAGES, n_dim * rows, cut), BF),
            pltpu.VMEM((STAGES, n_fact * rows, cut), F32),
            pltpu.VMEM((STAGES, n_fact, rows, cut), BF),
            pltpu.VMEM((STAGES, n_fact, rows, cut), BF),
            pltpu.VMEM((STAGES, rows, cut), BF),
            pltpu.VMEM((held, n_dim * rows, cut), BF),
            pltpu.VMEM((held, (tables + 1) * depth, cut), F32),
            pltpu.VMEM((held, n_fact, part, cut), BF),
            pltpu.VMEM((held, n_fact, part, cut), BF),
            *sems(n_fact),
            *[pltpu.SemaphoreType.DMA((n_dim,))] * 2,
            *sems(chips), *sems(chips), *sems(chips), *sems(chips),
            *sems(n_fact),
            pltpu.SemaphoreType.DMA((STAGES, chips)),
            pltpu.SemaphoreType.DMA((STAGES, chips, CORES)),
            *sems(n_fact), *sems(n_fact),
            *sems(n_fact, chips), *sems(n_fact, chips),
        ],
        compiler_params=pltpu.CompilerParams(
            collective_id=0, has_side_effects=True, vmem_limit_bytes=grant
        ),
        name="main",
    )(block_table, adj, w_one, facts, dims, cot, w_self)
    return pl.pallas_call(
        post_kernel,
        out_shape=(
            jax.ShapeDtypeStruct((rows, width), BF),
            jax.ShapeDtypeStruct((rows, width), F32),
            jax.ShapeDtypeStruct((width, width), F32),
            jax.ShapeDtypeStruct((tables, width, width), F32),
        ),
        in_specs=[vmem] * 3,
        out_specs=(anywhere,) * 4,
        scratch_shapes=[
            pltpu.VMEM((tables + 1, width, width), F32),
            pltpu.SemaphoreType.DMA((tables + 3,)),
        ],
        compiler_params=pltpu.CompilerParams(vmem_limit_bytes=12 << 20),
        name="post",
    )(fact_out, grad_dims, weights)


def solution(mesh):
    rows = P(("fact", "dim"), None)
    placed = (
        rows,
        rows,
        P(("fact", "dim"), None, None),
        rows,
        P(("fact", "dim")),
        P(),
        P(),
        P(),
        rows,
    )
    return jax.shard_map(
        body,
        mesh=mesh,
        in_specs=placed,
        out_specs=(rows, rows, P(), P()),
        check_vma=False,
    )
```

```python
import functools

import jax
import jax.numpy as jnp
from jax import lax
from jax.experimental import pallas as pl
from jax.experimental.pallas import tpu as pltpu
from jax.sharding import PartitionSpec as P

MESH = pl.DeviceIdType.MESH
BF = jnp.bfloat16
F32 = jnp.float32
CORES = 2
STAGES = 4


def dot(a, b):
    return jnp.dot(a, b, preferred_element_type=F32)


def flip(x):
    return x.astype(F32).T.astype(BF)


def prep_kernel(dims_n, links_h, count, table_h, tiles_h, w_tables_h, adj, w_one, links, table, tiles, acc, sems):
    n_fact, n_dim = dims_n
    chips = n_dim // CORES
    block = tiles.shape[1]
    f = lax.axis_index("fact")
    d = lax.axis_index("dim")
    small = [
        pltpu.make_async_copy(table_h, table, sems.at[0]),
        pltpu.make_async_copy(links_h, links, sems.at[1]),
    ]
    load = pltpu.make_async_copy(tiles_h, tiles, sems.at[2])
    for copy in small:
        copy.start()
    load.start()
    acc[...] = jnp.zeros_like(acc)
    small[0].wait()
    own = table[f * n_dim + d]
    weight = pltpu.make_async_copy(w_tables_h.at[own], w_one, sems.at[3])
    weight.start()
    small[1].wait()
    load.wait()

    def add(l, _):
        i = links[0, l] - f * n_dim
        row = lax.rem(i, CORES) * chips + lax.div(i, CORES)
        col = lax.div(links[1, l], n_dim)
        acc[row, col] += tiles[l].astype(F32)
        return 0

    lax.fori_loop(0, count[0], add, 0)
    for i in range(n_dim):
        for j in range(n_fact):
            adj[i * block : (i + 1) * block, j * block : (j + 1) * block] = acc[i, j].astype(BF)
    weight.wait()


def main_kernel(
    dims_n, table, adj, w_one, facts, dims, cot, w_self,
    fact_out, grad_dims, weights,
    proj, chunks, panel, adj_t, chunk_all, masked, pre, send1, recv1, mine, send2, recv2, gp, grad,
    send3, recv3, gs, gs_all, w_own, w_send, w_recv,
    sent, a_r, f_r, b1_r, b2_r, c_r, m_r, d_r, e_r, w_r, z_r, p_r, q_r,
):
    n_fact, n_dim = dims_n
    chips = n_dim // CORES
    rows, width = facts.shape
    cut = width // STAGES
    tables = weights.shape[1] - 1
    depth = chunks.shape[1] // 2
    per = n_fact // (tables + 1)
    part = depth // per
    f = lax.axis_index("fact")
    d = lax.axis_index("dim")
    c = lax.div(d, CORES)
    k = lax.rem(d, CORES)
    o = 1 - k
    mate = c * CORES + o
    scale_f = float(rows * n_fact * n_dim) ** -0.5
    to_f = [lax.rem(f + j, n_fact) for j in range(n_fact)]
    from_f = [lax.rem(f + n_fact - j, n_fact) for j in range(n_fact)]
    to_c = [lax.rem(c + j, chips) for j in range(chips)]
    from_c = [lax.rem(c + chips - j, chips) for j in range(chips)]
    every = range(STAGES)
    far = sorted(range(1, n_fact), key=lambda j: abs(2 * j - n_fact))
    near = sorted(range(1, n_fact), key=lambda j: min(j, n_fact - j))
    order = list(range(1, chips)) + [0]
    rb = k * chips + c
    group = chips * rows

    def remote(src, dst, ss, rs, df, dd):
        return pltpu.make_async_remote_copy(
            src_ref=src, dst_ref=dst, send_sem=ss, recv_sem=rs,
            device_id=(df, dd), device_id_type=MESH,
        )

    def arrive(ref, sem):
        pltpu.make_async_copy(ref, ref, sem).wait()

    def blk(i):
        return pl.ds(pl.multiple_of(i * rows, rows), rows)

    def grp(i):
        return pl.ds(pl.multiple_of(i * group, group), group)

    def unit(i):
        return pl.ds(pl.multiple_of(i * part, part), part)

    def cols(h):
        return slice(h * cut, (h + 1) * cut)

    def holder(h):
        return h % CORES

    def place(h, ff, cc):
        start = pl.multiple_of(cc * depth + lax.rem(ff, per) * part, part)
        return (h, lax.div(ff, per), pl.ds(start, part))

    def region(h, ff, cc):
        return weights.at[place(h, ff, cc)]

    def copy_a(h, j):
        return remote(proj.at[h], panel.at[h, blk(f)], sent.at[0], a_r.at[h], to_f[j], d)

    def copy_f(j):
        to = lax.rem(d + j, n_dim)
        return remote(
            chunks.at[lax.div(to, CORES)], chunk_all.at[:, blk(rb)], sent.at[1], f_r.at[0], f, to
        )

    def copy_1(h, j):
        at = blk(to_c[j])
        return remote(send1.at[h, at], recv1.at[h, at], sent.at[2], b1_r.at[h], f, mate)

    def copy_2(h, j):
        return remote(
            send2.at[h, j], recv2.at[h, j], sent.at[3], b2_r.at[h], f, to_c[j] * CORES + k
        )

    def copy_c(h, j):
        src = gp.at[h, blk(rb)]
        return remote(src, src, sent.at[4], c_r.at[h], f, to_c[j] * CORES + k)

    def copy_m(h, j):
        src = gp.at[h, blk(k * chips + from_c[j])]
        return remote(src, src, sent.at[5], m_r.at[h], f, mate)

    def copy_d(h, j):
        return remote(
            send3.at[h, j], recv3.at[h, j], sent.at[6], d_r.at[h], to_f[j], d
        )

    def copy_e(h, j):
        return remote(
            gs.at[h], gs_all.at[h // CORES, blk(rb)], sent.at[7], e_r.at[h],
            f, to_c[j] * CORES + holder(h),
        )

    def copy_w(h, j):
        return remote(
            w_send.at[h // CORES, j], w_recv.at[h // CORES, j], sent.at[8], w_r.at[h],
            to_f[j], d,
        )

    def copy_z(h, j):
        src = region(h, f, c)
        return remote(src, src, sent.at[9], z_r.at[h, j], to_f[j], d)

    def copy_p(h, i, j):
        src = region(h, from_f[i], c)
        return remote(src, src, sent.at[10], p_r.at[h, i], f, to_c[j] * CORES + k)

    def copy_q(h, i, j):
        src = region(h, from_f[i], from_c[j])
        return remote(src, src, sent.at[11], q_r.at[h], f, mate)

    barrier = pltpu.get_barrier_semaphore()
    for j in range(1, n_fact):
        pl.semaphore_signal(barrier, inc=1, device_id=(to_f[j], d), device_id_type=MESH)
    for j in range(1, n_dim):
        pl.semaphore_signal(
            barrier, inc=1, device_id=(f, lax.rem(d + j, n_dim)), device_id_type=MESH
        )
    both = dot(dims[...], w_one[...]).astype(BF)
    for h in every:
        proj[h] = both[:, cols(h)]
    pl.semaphore_wait(barrier, n_dim + n_fact - 2)

    for h in every:
        for j in far:
            copy_a(h, j).start()
    facts_t = flip(facts[...])
    dims_t = flip(dims[...])
    for i in range(chips):
        chunks[i, :depth] = facts_t[i * depth : (i + 1) * depth]
        chunks[i, depth:] = dims_t[i * depth : (i + 1) * depth]
    for j in range(1, n_dim):
        copy_f(j).start()
    for h in every:
        panel[h, blk(f), :] = proj[h]
        pre[h] = dot(facts[...], w_self[:, cols(h)])
    chunk_all[:, blk(rb)] = chunks[c]
    for i in range(n_dim):
        adj_t[:, i * rows : (i + 1) * rows] = flip(adj[i * rows : (i + 1) * rows, :])

    def forward(h):
        arrive(panel.at[h, pl.ds(rows, (n_fact - 1) * rows)], a_r.at[h])
        send1[h] = dot(adj[grp(o), :], panel[h]).astype(BF)
        for j in order:
            copy_1(h, j).start()
        mine[h] = dot(adj[grp(k), :], panel[h])

    def pair(h):
        arrive(recv1.at[h], b1_r.at[h])
        for j in order:
            at = blk(to_c[j])
            total = mine[h, at, :] + recv1[h, at, :].astype(F32)
            if j:
                send2[h, j] = total.astype(BF)
                copy_2(h, j).start()
            else:
                pre[h] += total

    def activate(h):
        total = pre[h]
        arrive(recv2.at[h, pl.ds(1, chips - 1)], b2_r.at[h])
        for j in range(1, chips):
            total = total + recv2[h, j].astype(F32)
        sig = 1.0 / (1.0 + jnp.exp(-total))
        gp[h, blk(rb), :] = (
            cot[:, cols(h)].astype(F32) * sig * (1.0 + total * (1.0 - sig))
        ).astype(BF)
        for j in range(1, chips):
            copy_c(h, j).start()
        copy_m(h, 0).start()
        fact_out[:, cols(h)] = (total * sig).astype(BF)

    def share(h):
        arrive(recv2.at[h, pl.ds(1, chips - 1)], c_r.at[h])
        for j in range(1, chips):
            copy_m(h, j).start()
        grad[h] = dot(adj_t[:, grp(k)], gp[h, grp(k), :])

    def mask():
        arrive(chunk_all.at[:, pl.ds(rows, (n_dim - 1) * rows)], f_r.at[0])
        for i in range(n_dim):
            source = (i % chips) * CORES + i // chips
            name = table[f * n_dim + source]
            lanes = slice(i * rows, (i + 1) * rows)
            values = chunk_all[depth:, lanes].astype(F32)
            for t in range(tables):
                masked[t * depth : (t + 1) * depth, lanes] = (
                    values * (name == t).astype(F32)
                ).astype(BF)

    def backward(h):
        arrive(gp.at[h, pl.ds(0, group)], m_r.at[h])
        grad[h] += dot(adj_t[:, grp(o)], gp[h, grp(o), :])
        for j in far:
            send3[h, j] = grad[h, blk(to_f[j]), :].astype(BF)
            copy_d(h, j).start()

        @pl.when(k == holder(h))
        def _():
            w_own[h // CORES, :depth, :] = dot(chunk_all[:depth, :], gp[h]) * scale_f

    def collect(h):
        total = grad[h, blk(f), :]
        arrive(recv3.at[h, pl.ds(1, n_fact - 1)], d_r.at[h])
        for j in near:
            total = total + recv3[h, j].astype(F32)
        rounded = total.astype(BF)
        gs[h] = rounded
        for j in range(1, chips):
            copy_e(h, j).start()

        @pl.when(k != holder(h))
        def _():
            copy_e(h, 0).start()

        @pl.when(k == holder(h))
        def _():
            gs_all[h // CORES, blk(rb), :] = gs[h]

        term = lax.dot_general(
            rounded, w_one[:, cols(h)], (((1,), (1,)), ((), ())), preferred_element_type=F32
        )
        if h:
            grad_dims[...] += term
        else:
            grad_dims[...] = term

    def table_weight(h):
        @pl.when(k == holder(h))
        def _():
            own = h // CORES
            arrive(gs_all.at[own, pl.ds(rows, (n_dim - 1) * rows)], e_r.at[h])
            w_own[own, depth:, :] = dot(masked[...], gs_all[own]) * scale_f
            for j in far:
                w_send[own, j] = w_own[own, unit(to_f[j]), :].astype(BF)
                copy_w(h, j).start()

    def finish(h):
        @pl.when(k == holder(h))
        def _():
            own = h // CORES
            total = w_own[own, unit(f), :]
            arrive(w_recv.at[own, pl.ds(1, n_fact - 1)], w_r.at[h])
            for j in near:
                total = total + w_recv[own, j].astype(F32)
            weights[place(h, f, c)] = total.astype(BF)
            for j in far:
                copy_z(h, j).start()
            for j in range(1, chips):
                copy_p(h, 0, j).start()
            copy_q(h, 0, 0).start()

    def relay(h):
        @pl.when(k == holder(h))
        def _():
            for i in near:
                arrive(region(h, f, c), z_r.at[h, i])
                for j in range(1, chips):
                    copy_p(h, i, j).start()
                copy_q(h, i, 0).start()

    def hand(h):
        @pl.when(k == holder(h))
        def _():
            for i in [0] + near:
                arrive(weights.at[h, 0, pl.ds(0, (chips - 1) * part)], p_r.at[h, i])
                for j in range(1, chips):
                    copy_q(h, i, j).start()

    tasks = [
        (0.0, forward), (1.5, pair), (5.2, activate), (8.8, share), (9.9, backward),
        (15.4, collect), (19.1, table_weight), (23.4, finish), (27.4, relay), (32.0, hand),
    ]
    step = 2.5
    plan = [(at + step * h, h, task) for at, task in tasks for h in every]
    plan.append((6.0, 0, lambda h: mask()))
    for _, h, task in sorted(plan, key=lambda item: item[:2]):
        task(h)

    for h in every:
        @pl.when(k != holder(h))
        def _():
            arrive(weights.at[h], q_r.at[h])

    held = STAGES // CORES
    for i, ref in enumerate((
        panel.at[:, pl.ds(rows, (n_fact - 1) * rows)],
        chunk_all.at[:, pl.ds(rows, (n_dim - 1) * rows)],
        send1,
        send2.at[:, pl.ds(1, chips - 1)],
        send2.at[:, pl.ds(1, chips - 1)],
        send1,
        send3.at[:, pl.ds(1, n_fact - 1)],
        gs_all.at[:, pl.ds(rows, (n_dim - 1) * rows)],
        w_send.at[:, pl.ds(1, n_fact - 1)],
        w_send.at[:, pl.ds(1, n_fact - 1)],
        weights.at[pl.ds(0, held), :, pl.ds(0, width - depth)],
        weights.at[pl.ds(0, held)],
    )):
        arrive(ref, sent.at[i])


def post_kernel(out_in, dims_in, weights, fact_out, grad_dims, w_self, w_tables, wide, sems):
    stages, tables, _, cut = weights.shape
    started = [
        pltpu.make_async_copy(out_in, fact_out, sems.at[tables]),
        pltpu.make_async_copy(dims_in, grad_dims, sems.at[tables + 1]),
    ]
    for copy in started:
        copy.start()
    for t in range(tables):
        for h in range(stages):
            wide[t, :, h * cut : (h + 1) * cut] = weights[h, t].astype(F32)
        copy = pltpu.make_async_copy(
            wide.at[t], w_tables.at[t - 1] if t else w_self, sems.at[t]
        )
        copy.start()
        started.append(copy)
    for copy in started:
        copy.wait()


def body(facts, dims, tiles, links, link_count, block_table, w_self, w_tables, cot):
    n_fact = lax.axis_size("fact")
    n_dim = lax.axis_size("dim")
    chips = n_dim // CORES
    rows, width = facts.shape
    block = tiles.shape[1]
    tables = w_tables.shape[0]
    depth = width // chips
    cut = width // STAGES
    part = depth * (tables + 1) // n_fact
    dims_n = (n_fact, n_dim)
    cells = n_fact * n_dim * rows * rows
    panes = (n_fact + n_dim) * rows * width
    grant = min(62 << 20, 4 * cells + 16 * panes + 8 * tables * width * width + (6 << 20))
    small = min(62 << 20, 8 * cells + 4 * width * width + 2 * tiles.size + (4 << 20))
    vmem = pl.BlockSpec(memory_space=pltpu.VMEM)
    smem = pl.BlockSpec(memory_space=pltpu.SMEM)
    anywhere = pl.BlockSpec(memory_space=pl.ANY)
    hbm = pl.BlockSpec(memory_space=pltpu.HBM)

    def stay(x):
        return pltpu.with_memory_space_constraint(x, pltpu.HBM)

    adj, w_one = pl.pallas_call(
        functools.partial(prep_kernel, dims_n),
        out_shape=(
            jax.ShapeDtypeStruct((n_dim * rows, n_fact * rows), BF),
            jax.ShapeDtypeStruct((width, width), BF),
        ),
        in_specs=[hbm, smem, hbm, hbm, hbm],
        out_specs=(vmem, vmem),
        scratch_shapes=[
            pltpu.SMEM(links.shape[::-1], jnp.int32),
            pltpu.SMEM(block_table.shape, jnp.int32),
            pltpu.VMEM(tiles.shape, BF),
            pltpu.VMEM((n_dim, n_fact, block, block), F32),
            pltpu.SemaphoreType.DMA((4,)),
        ],
        compiler_params=pltpu.CompilerParams(vmem_limit_bytes=small),
        name="prep",
    )(stay(links.T), link_count, stay(block_table), stay(tiles), stay(w_tables))

    def sems(*shape):
        return pltpu.SemaphoreType.DMA(shape)

    held = STAGES // CORES
    fact_out, grad_dims, weights = pl.pallas_call(
        functools.partial(main_kernel, dims_n),
        out_shape=(
            jax.ShapeDtypeStruct((rows, width), BF),
            jax.ShapeDtypeStruct((rows, width), F32),
            jax.ShapeDtypeStruct((STAGES, tables + 1, width, cut), BF),
        ),
        in_specs=[smem] + [vmem] * 6,
        out_specs=(vmem, vmem, vmem),
        scratch_shapes=[
            pltpu.VMEM((STAGES, rows, cut), BF),
            pltpu.VMEM((chips, 2 * depth, rows), BF),
            pltpu.VMEM((STAGES, n_fact * rows, cut), BF),
            pltpu.VMEM((n_fact * rows, n_dim * rows), BF),
            pltpu.VMEM((2 * depth, n_dim * rows), BF),
            pltpu.VMEM((tables * depth, n_dim * rows), BF),
            pltpu.VMEM((STAGES, rows, cut), F32),
            pltpu.VMEM((STAGES, chips * rows, cut), BF),
            pltpu.VMEM((STAGES, chips * rows, cut), BF),
            pltpu.VMEM((STAGES, chips * rows, cut), F32),
            pltpu.VMEM((STAGES, chips, rows, cut), BF),
            pltpu.VMEM((STAGES, chips, rows, cut), BF),
            pltpu.VMEM((STAGES, n_dim * rows, cut), BF),
            pltpu.VMEM((STAGES, n_fact * rows, cut), F32),
            pltpu.VMEM((STAGES, n_fact, rows, cut), BF),
            pltpu.VMEM((STAGES, n_fact, rows, cut), BF),
            pltpu.VMEM((STAGES, rows, cut), BF),
            pltpu.VMEM((held, n_dim * rows, cut), BF),
            pltpu.VMEM((held, (tables + 1) * depth, cut), F32),
            pltpu.VMEM((held, n_fact, part, cut), BF),
            pltpu.VMEM((held, n_fact, part, cut), BF),
            sems(12), sems(STAGES), sems(1),
            *[sems(STAGES)] * 7,
            sems(STAGES, n_fact), sems(STAGES, n_fact), sems(STAGES),
        ],
        compiler_params=pltpu.CompilerParams(
            collective_id=0, has_side_effects=True, vmem_limit_bytes=grant
        ),
        name="main",
    )(block_table, adj, w_one, facts, dims, cot, w_self)
    return pl.pallas_call(
        post_kernel,
        out_shape=(
            jax.ShapeDtypeStruct((rows, width), BF),
            jax.ShapeDtypeStruct((rows, width), F32),
            jax.ShapeDtypeStruct((width, width), F32),
            jax.ShapeDtypeStruct((tables, width, width), F32),
        ),
        in_specs=[vmem] * 3,
        out_specs=(anywhere,) * 4,
        scratch_shapes=[
            pltpu.VMEM((tables + 1, width, width), F32),
            pltpu.SemaphoreType.DMA((tables + 3,)),
        ],
        compiler_params=pltpu.CompilerParams(vmem_limit_bytes=12 << 20),
        name="post",
    )(fact_out, grad_dims, weights)


def solution(mesh):
    rows = P(("fact", "dim"), None)
    placed = (
        rows,
        rows,
        P(("fact", "dim"), None, None),
        rows,
        P(("fact", "dim")),
        P(),
        P(),
        P(),
        rows,
    )
    return jax.shard_map(
        body,
        mesh=mesh,
        in_specs=placed,
        out_specs=(rows, rows, P(), P()),
        check_vma=False,
    )
```

```python
import functools

import jax
import jax.numpy as jnp
from jax import lax
from jax.experimental import pallas as pl
from jax.experimental.pallas import tpu as pltpu
from jax.sharding import PartitionSpec as P

MESH = pl.DeviceIdType.MESH
BF = jnp.bfloat16
F32 = jnp.float32
CORES = 2
STAGES = 4


def dot(a, b):
    return jnp.dot(a, b, preferred_element_type=F32)


def flip(x):
    return x.astype(F32).T.astype(BF)


def prep_kernel(dims_n, links_h, count, table_h, tiles_h, w_tables_h, adj, w_one, names, links, table, tiles, acc, sems):
    n_fact, n_dim = dims_n
    chips = n_dim // CORES
    block = tiles.shape[1]
    f = lax.axis_index("fact")
    d = lax.axis_index("dim")
    small = [
        pltpu.make_async_copy(table_h, table, sems.at[0]),
        pltpu.make_async_copy(links_h, links, sems.at[1]),
    ]
    load = pltpu.make_async_copy(tiles_h, tiles, sems.at[2])
    for copy in small:
        copy.start()
    load.start()
    acc[...] = jnp.zeros_like(acc)
    small[0].wait()
    own = table[f * n_dim + d]
    weight = pltpu.make_async_copy(w_tables_h.at[own], w_one, sems.at[3])
    weight.start()
    for i in range(n_dim):
        source = (i % chips) * CORES + i // chips
        name = table[f * n_dim + source].astype(F32)
        names[i : i + 1, :] = jnp.full((1, names.shape[1]), name, F32)
    small[1].wait()
    load.wait()

    def add(l, _):
        i = links[0, l] - f * n_dim
        row = lax.rem(i, CORES) * chips + lax.div(i, CORES)
        col = lax.div(links[1, l], n_dim)
        acc[row, col] += tiles[l].astype(F32)
        return 0

    lax.fori_loop(0, count[0], add, 0)
    for i in range(n_dim):
        for j in range(n_fact):
            adj[i * block : (i + 1) * block, j * block : (j + 1) * block] = acc[i, j].astype(BF)
    weight.wait()


def main_kernel(
    dims_n, names, adj, w_one, facts, dims, cot, w_self,
    fact_out, grad_dims, weights,
    proj, chunks, panel, adj_t, chunk_all, masked, pre, send1, recv1, mine, send2, recv2, gp, grad,
    send3, recv3, gs, gs_all, w_own, w_send, w_recv,
    sent, a_r, f_r, b1_r, b2_r, c_r, m_r, d_r, e_r, w_r, z_r, p_r, q_r,
):
    n_fact, n_dim = dims_n
    chips = n_dim // CORES
    rows, width = facts.shape
    cut = width // STAGES
    tables = weights.shape[1] - 1
    depth = chunks.shape[1] // 2
    per = n_fact // (tables + 1)
    part = depth // per
    f = lax.axis_index("fact")
    d = lax.axis_index("dim")
    c = lax.div(d, CORES)
    k = lax.rem(d, CORES)
    o = 1 - k
    mate = c * CORES + o
    scale_f = float(rows * n_fact * n_dim) ** -0.5
    to_f = [lax.rem(f + j, n_fact) for j in range(n_fact)]
    from_f = [lax.rem(f + n_fact - j, n_fact) for j in range(n_fact)]
    to_c = [lax.rem(c + j, chips) for j in range(chips)]
    from_c = [lax.rem(c + chips - j, chips) for j in range(chips)]
    every = range(STAGES)
    far = sorted(range(1, n_fact), key=lambda j: abs(2 * j - n_fact))
    near = sorted(range(1, n_fact), key=lambda j: min(j, n_fact - j))
    order = list(range(1, chips)) + [0]
    rb = k * chips + c
    group = chips * rows

    def remote(src, dst, ss, rs, df, dd):
        return pltpu.make_async_remote_copy(
            src_ref=src, dst_ref=dst, send_sem=ss, recv_sem=rs,
            device_id=(df, dd), device_id_type=MESH,
        )

    def arrive(ref, sem):
        pltpu.make_async_copy(ref, ref, sem).wait()

    def blk(i):
        return pl.ds(pl.multiple_of(i * rows, rows), rows)

    def grp(i):
        return pl.ds(pl.multiple_of(i * group, group), group)

    def unit(i):
        return pl.ds(pl.multiple_of(i * part, part), part)

    def cols(h):
        return slice(h * cut, (h + 1) * cut)

    def holder(h):
        return h % CORES

    def place(h, ff, cc):
        start = pl.multiple_of(cc * depth + lax.rem(ff, per) * part, part)
        return (h, lax.div(ff, per), pl.ds(start, part))

    def region(h, ff, cc):
        return weights.at[place(h, ff, cc)]

    def copy_a(h, j):
        return remote(proj.at[h], panel.at[h, blk(f)], sent.at[0], a_r.at[h], to_f[j], d)

    def copy_f(j):
        to = lax.rem(d + j, n_dim)
        return remote(
            chunks.at[lax.div(to, CORES)], chunk_all.at[:, blk(rb)], sent.at[1], f_r.at[0], f, to
        )

    def copy_1(h, j):
        at = blk(to_c[j])
        return remote(send1.at[h, at], recv1.at[h, at], sent.at[2], b1_r.at[h], f, mate)

    def copy_2(h, j):
        return remote(
            send2.at[h, j], recv2.at[h, j], sent.at[3], b2_r.at[h], f, to_c[j] * CORES + k
        )

    def copy_c(h, j):
        src = gp.at[h, blk(rb)]
        return remote(src, src, sent.at[4], c_r.at[h], f, to_c[j] * CORES + k)

    def copy_m(h, j):
        src = gp.at[h, blk(k * chips + from_c[j])]
        return remote(src, src, sent.at[5], m_r.at[h], f, mate)

    def copy_d(h, j):
        return remote(
            send3.at[h, j], recv3.at[h, j], sent.at[6], d_r.at[h], to_f[j], d
        )

    def copy_e(h, j):
        return remote(
            gs.at[h], gs_all.at[h // CORES, blk(rb)], sent.at[7], e_r.at[h],
            f, to_c[j] * CORES + holder(h),
        )

    def copy_w(h, j):
        return remote(
            w_send.at[h // CORES, j], w_recv.at[h // CORES, j], sent.at[8], w_r.at[h],
            to_f[j], d,
        )

    def copy_z(h, j):
        src = region(h, f, c)
        return remote(src, src, sent.at[9], z_r.at[h, j], to_f[j], d)

    def copy_p(h, i, j):
        src = region(h, from_f[i], c)
        return remote(src, src, sent.at[10], p_r.at[h, i], f, to_c[j] * CORES + k)

    def copy_q(h, i, j):
        src = region(h, from_f[i], from_c[j])
        return remote(src, src, sent.at[11], q_r.at[h], f, mate)

    barrier = pltpu.get_barrier_semaphore()
    for j in range(1, n_fact):
        pl.semaphore_signal(barrier, inc=1, device_id=(to_f[j], d), device_id_type=MESH)
    for j in range(1, n_dim):
        pl.semaphore_signal(
            barrier, inc=1, device_id=(f, lax.rem(d + j, n_dim)), device_id_type=MESH
        )
    both = dot(dims[...], w_one[...]).astype(BF)
    for h in every:
        proj[h] = both[:, cols(h)]
    pl.semaphore_wait(barrier, n_dim + n_fact - 2)

    for h in every:
        for j in far:
            copy_a(h, j).start()
    facts_t = flip(facts[...])
    dims_t = flip(dims[...])
    for i in range(chips):
        chunks[i, :depth] = facts_t[i * depth : (i + 1) * depth]
        chunks[i, depth:] = dims_t[i * depth : (i + 1) * depth]
    for j in range(1, n_dim):
        copy_f(j).start()
    for h in every:
        panel[h, blk(f), :] = proj[h]
        pre[h] = dot(facts[...], w_self[:, cols(h)])
    chunk_all[:, blk(rb)] = chunks[c]
    for i in range(n_dim):
        adj_t[:, i * rows : (i + 1) * rows] = flip(adj[i * rows : (i + 1) * rows, :])

    def forward(h):
        arrive(panel.at[h, pl.ds(rows, (n_fact - 1) * rows)], a_r.at[h])
        send1[h] = dot(adj[grp(o), :], panel[h]).astype(BF)
        for j in order:
            copy_1(h, j).start()
        mine[h] = dot(adj[grp(k), :], panel[h])

    def pair(h):
        arrive(recv1.at[h], b1_r.at[h])
        for j in order:
            at = blk(to_c[j])
            total = mine[h, at, :] + recv1[h, at, :].astype(F32)
            if j:
                send2[h, j] = total.astype(BF)
                copy_2(h, j).start()
            else:
                pre[h] += total

    def activate(h):
        total = pre[h]
        arrive(recv2.at[h, pl.ds(1, chips - 1)], b2_r.at[h])
        for j in range(1, chips):
            total = total + recv2[h, j].astype(F32)
        sig = 1.0 / (1.0 + jnp.exp(-total))
        gp[h, blk(rb), :] = (
            cot[:, cols(h)].astype(F32) * sig * (1.0 + total * (1.0 - sig))
        ).astype(BF)
        for j in range(1, chips):
            copy_c(h, j).start()
        copy_m(h, 0).start()
        fact_out[:, cols(h)] = (total * sig).astype(BF)

    def share(h):
        arrive(recv2.at[h, pl.ds(1, chips - 1)], c_r.at[h])
        for j in range(1, chips):
            copy_m(h, j).start()
        grad[h] = dot(adj_t[:, grp(k)], gp[h, grp(k), :])

    def mask():
        arrive(chunk_all.at[:, pl.ds(rows, (n_dim - 1) * rows)], f_r.at[0])
        for i in range(n_dim):
            name = names[i : i + 1, :]
            lanes = slice(i * rows, (i + 1) * rows)
            values = chunk_all[depth:, lanes].astype(F32)
            for t in range(tables):
                masked[t * depth : (t + 1) * depth, lanes] = (
                    values * (name == t).astype(F32)
                ).astype(BF)

    def backward(h):
        arrive(gp.at[h, pl.ds(0, group)], m_r.at[h])
        grad[h] += dot(adj_t[:, grp(o)], gp[h, grp(o), :])
        for j in far:
            send3[h, j] = grad[h, blk(to_f[j]), :].astype(BF)
            copy_d(h, j).start()

        @pl.when(k == holder(h))
        def _():
            w_own[h // CORES, :depth, :] = dot(chunk_all[:depth, :], gp[h]) * scale_f

    def collect(h):
        total = grad[h, blk(f), :]
        arrive(recv3.at[h, pl.ds(1, n_fact - 1)], d_r.at[h])
        for j in near:
            total = total + recv3[h, j].astype(F32)
        rounded = total.astype(BF)
        gs[h] = rounded
        for j in range(1, chips):
            copy_e(h, j).start()

        @pl.when(k != holder(h))
        def _():
            copy_e(h, 0).start()

        @pl.when(k == holder(h))
        def _():
            gs_all[h // CORES, blk(rb), :] = gs[h]

        term = lax.dot_general(
            rounded, w_one[:, cols(h)], (((1,), (1,)), ((), ())), preferred_element_type=F32
        )
        if h:
            grad_dims[...] += term
        else:
            grad_dims[...] = term

    def table_weight(h):
        @pl.when(k == holder(h))
        def _():
            own = h // CORES
            arrive(gs_all.at[own, pl.ds(rows, (n_dim - 1) * rows)], e_r.at[h])
            w_own[own, depth:, :] = dot(masked[...], gs_all[own]) * scale_f
            for j in far:
                w_send[own, j] = w_own[own, unit(to_f[j]), :].astype(BF)
                copy_w(h, j).start()

    def finish(h):
        @pl.when(k == holder(h))
        def _():
            own = h // CORES
            total = w_own[own, unit(f), :]
            arrive(w_recv.at[own, pl.ds(1, n_fact - 1)], w_r.at[h])
            for j in near:
                total = total + w_recv[own, j].astype(F32)
            weights[place(h, f, c)] = total.astype(BF)
            for j in far:
                copy_z(h, j).start()
            for j in range(1, chips):
                copy_p(h, 0, j).start()
            copy_q(h, 0, 0).start()

    def relay(h):
        @pl.when(k == holder(h))
        def _():
            for i in near:
                arrive(region(h, f, c), z_r.at[h, i])
                for j in range(1, chips):
                    copy_p(h, i, j).start()
                copy_q(h, i, 0).start()

    def hand(h):
        @pl.when(k == holder(h))
        def _():
            for i in [0] + near:
                arrive(weights.at[h, 0, pl.ds(0, (chips - 1) * part)], p_r.at[h, i])
                for j in range(1, chips):
                    copy_q(h, i, j).start()

    tasks = [
        (0.0, 3.2, forward), (1.5, 3.2, pair), (6.4, 3.2, activate), (10.0, 3.2, share),
        (11.1, 3.7, backward), (16.6, 3.7, collect), (20.3, 3.7, table_weight),
        (24.6, 3.7, finish), (28.6, 3.7, relay), (33.2, 3.7, hand),
    ]
    plan = [(at + step * h, h, task) for at, step, task in tasks for h in every]
    plan.append((6.0, 0, lambda h: mask()))
    for _, h, task in sorted(plan, key=lambda item: item[:2]):
        task(h)

    for h in every:
        @pl.when(k != holder(h))
        def _():
            arrive(weights.at[h], q_r.at[h])

    held = STAGES // CORES
    for i, ref in enumerate((
        panel.at[:, pl.ds(rows, (n_fact - 1) * rows)],
        chunk_all.at[:, pl.ds(rows, (n_dim - 1) * rows)],
        send1,
        send2.at[:, pl.ds(1, chips - 1)],
        send2.at[:, pl.ds(1, chips - 1)],
        send1,
        send3.at[:, pl.ds(1, n_fact - 1)],
        gs_all.at[:, pl.ds(rows, (n_dim - 1) * rows)],
        w_send.at[:, pl.ds(1, n_fact - 1)],
        w_send.at[:, pl.ds(1, n_fact - 1)],
        weights.at[pl.ds(0, held), :, pl.ds(0, width - depth)],
        weights.at[pl.ds(0, held)],
    )):
        arrive(ref, sent.at[i])


def post_kernel(out_in, dims_in, weights, fact_out, grad_dims, w_self, w_tables, wide, sems):
    stages, tables, _, cut = weights.shape
    started = [
        pltpu.make_async_copy(out_in, fact_out, sems.at[tables]),
        pltpu.make_async_copy(dims_in, grad_dims, sems.at[tables + 1]),
    ]
    for copy in started:
        copy.start()
    for t in range(tables):
        target = w_tables.at[t - 1] if t else w_self
        for h in range(stages):
            lanes = pl.ds(h * cut, cut)
            wide[t, :, lanes] = weights[h, t].astype(F32)
            pltpu.make_async_copy(wide.at[t, :, lanes], target.at[:, lanes], sems.at[t]).start()
        started.append(pltpu.make_async_copy(wide.at[t], target, sems.at[t]))
    for copy in started:
        copy.wait()


def body(facts, dims, tiles, links, link_count, block_table, w_self, w_tables, cot):
    n_fact = lax.axis_size("fact")
    n_dim = lax.axis_size("dim")
    chips = n_dim // CORES
    rows, width = facts.shape
    block = tiles.shape[1]
    tables = w_tables.shape[0]
    depth = width // chips
    cut = width // STAGES
    part = depth * (tables + 1) // n_fact
    dims_n = (n_fact, n_dim)
    cells = n_fact * n_dim * rows * rows
    panes = (n_fact + n_dim) * rows * width
    grant = min(62 << 20, 4 * cells + 16 * panes + 8 * tables * width * width + (6 << 20))
    small = min(62 << 20, 8 * cells + 4 * width * width + 2 * tiles.size + (4 << 20))
    vmem = pl.BlockSpec(memory_space=pltpu.VMEM)
    smem = pl.BlockSpec(memory_space=pltpu.SMEM)
    anywhere = pl.BlockSpec(memory_space=pl.ANY)
    hbm = pl.BlockSpec(memory_space=pltpu.HBM)

    def stay(x):
        return pltpu.with_memory_space_constraint(x, pltpu.HBM)

    adj, w_one, names = pl.pallas_call(
        functools.partial(prep_kernel, dims_n),
        out_shape=(
            jax.ShapeDtypeStruct((n_dim * rows, n_fact * rows), BF),
            jax.ShapeDtypeStruct((width, width), BF),
            jax.ShapeDtypeStruct((n_dim, rows), F32),
        ),
        in_specs=[hbm, smem, hbm, hbm, hbm],
        out_specs=(vmem, vmem, vmem),
        scratch_shapes=[
            pltpu.SMEM(links.shape[::-1], jnp.int32),
            pltpu.SMEM(block_table.shape, jnp.int32),
            pltpu.VMEM(tiles.shape, BF),
            pltpu.VMEM((n_dim, n_fact, block, block), F32),
            pltpu.SemaphoreType.DMA((4,)),
        ],
        compiler_params=pltpu.CompilerParams(vmem_limit_bytes=small),
        name="prep",
    )(stay(links.T), link_count, stay(block_table), stay(tiles), stay(w_tables))

    def sems(*shape):
        return pltpu.SemaphoreType.DMA(shape)

    held = STAGES // CORES
    fact_out, grad_dims, weights = pl.pallas_call(
        functools.partial(main_kernel, dims_n),
        out_shape=(
            jax.ShapeDtypeStruct((rows, width), BF),
            jax.ShapeDtypeStruct((rows, width), F32),
            jax.ShapeDtypeStruct((STAGES, tables + 1, width, cut), BF),
        ),
        in_specs=[vmem] * 7,
        out_specs=(vmem, vmem, vmem),
        scratch_shapes=[
            pltpu.VMEM((STAGES, rows, cut), BF),
            pltpu.VMEM((chips, 2 * depth, rows), BF),
            pltpu.VMEM((STAGES, n_fact * rows, cut), BF),
            pltpu.VMEM((n_fact * rows, n_dim * rows), BF),
            pltpu.VMEM((2 * depth, n_dim * rows), BF),
            pltpu.VMEM((tables * depth, n_dim * rows), BF),
            pltpu.VMEM((STAGES, rows, cut), F32),
            pltpu.VMEM((STAGES, chips * rows, cut), BF),
            pltpu.VMEM((STAGES, chips * rows, cut), BF),
            pltpu.VMEM((STAGES, chips * rows, cut), F32),
            pltpu.VMEM((STAGES, chips, rows, cut), BF),
            pltpu.VMEM((STAGES, chips, rows, cut), BF),
            pltpu.VMEM((STAGES, n_dim * rows, cut), BF),
            pltpu.VMEM((STAGES, n_fact * rows, cut), F32),
            pltpu.VMEM((STAGES, n_fact, rows, cut), BF),
            pltpu.VMEM((STAGES, n_fact, rows, cut), BF),
            pltpu.VMEM((STAGES, rows, cut), BF),
            pltpu.VMEM((held, n_dim * rows, cut), BF),
            pltpu.VMEM((held, (tables + 1) * depth, cut), F32),
            pltpu.VMEM((held, n_fact, part, cut), BF),
            pltpu.VMEM((held, n_fact, part, cut), BF),
            sems(12), sems(STAGES), sems(1),
            *[sems(STAGES)] * 7,
            sems(STAGES, n_fact), sems(STAGES, n_fact), sems(STAGES),
        ],
        compiler_params=pltpu.CompilerParams(
            collective_id=0, has_side_effects=True, vmem_limit_bytes=grant
        ),
        name="main",
    )(names, adj, w_one, facts, dims, cot, w_self)
    return pl.pallas_call(
        post_kernel,
        out_shape=(
            jax.ShapeDtypeStruct((rows, width), BF),
            jax.ShapeDtypeStruct((rows, width), F32),
            jax.ShapeDtypeStruct((width, width), F32),
            jax.ShapeDtypeStruct((tables, width, width), F32),
        ),
        in_specs=[vmem] * 3,
        out_specs=(anywhere,) * 4,
        scratch_shapes=[
            pltpu.VMEM((tables + 1, width, width), F32),
            pltpu.SemaphoreType.DMA((tables + 3,)),
        ],
        compiler_params=pltpu.CompilerParams(vmem_limit_bytes=12 << 20),
        name="post",
    )(fact_out, grad_dims, weights)


def solution(mesh):
    rows = P(("fact", "dim"), None)
    placed = (
        rows,
        rows,
        P(("fact", "dim"), None, None),
        rows,
        P(("fact", "dim")),
        P(),
        P(),
        P(),
        rows,
    )
    return jax.shard_map(
        body,
        mesh=mesh,
        in_specs=placed,
        out_specs=(rows, rows, P(), P()),
        check_vma=False,
    )
```
